32 devices in a mesh: win: 16 (over z, y, x), strip: 2 (over core).
Axes of the slice: x: 2, y: 2, z: 4, core: 2. Of those that a mesh axis runs over, the one named last changes fastest.
Arguments:
- start_states: float32 [16, 3, 32, 1024], P('win', None, 'strip'), may hold values from -1.5 to 1.5
- obs_cells: int32 [16, 4, 512], P('win', None, 'strip'), may hold values from 0 to 16383
- obs_values: float32 [16, 4, 512], P('win', None, 'strip'), may hold values from -1.5 to 1.5
- weighting: float32 [3, 128, 128], replicated, may hold values from -0.5 to 0.5
- live_windows: int32 [16], P('win'), may hold values 0 or 1
Outputs:
- gradient: float32 [16, 3, 32, 1024], P('win', None, 'strip')
- analysis: float32 [16, 3, 32, 1024], P('win', None, 'strip')
The draws below stay inside these ranges and needn't reach their ends.
Inputs may be any that keep to these rules, and one draw needn't show every extreme that they name: `obs_cells`: each entry indexes a cell of its own row strip as (row within the strip) * 1024 + column.
All inputs are finite; a program needn't handle non-finite values. No bound on the sum of `live_windows` on one device may be relied on, other than what follows from the above.
Results may differ from the reference program's by a relative error of at most 0.0003.
Values sent between devices are 32-bit elements; how exact they have to be, the bound alone decides.
A program may use at most 64 MiB of HBM per device.

```python
import jax
import jax.numpy as jnp
from jax import lax

COLS = 1024
BLOCK = 128
ROWS_DEV = 16
STEPS = 4
OBS = 256
WINDOWS = 16
NROWS = 32
N_STRIP = 2


def place_ends(entries, key, least, largest):
    dims = entries.shape
    index_at = [jax.random.randint(jax.random.fold_in(key, axis), (), 0, dims[axis]) for axis in range(len(dims))]
    entries = entries.at[tuple(index_at)].set(least)
    longest = dims.index(max(dims))
    index_at[longest] = (index_at[longest] + 1) % dims[longest]
    return entries.at[tuple(index_at)].set(largest)


def shard_levels(stream_key, dims, pieces, low, high):
    gain, own = 1.0, jax.random.fold_in(stream_key, 6)
    for dim, shards_of in pieces:
        steps = jnp.exp(jax.random.uniform(jax.random.fold_in(own, dim), (shards_of,), jnp.float32, low / len(pieces), high / len(pieces)))
        gain = gain * jnp.repeat(steps, dims[dim] // shards_of).reshape([-1 if axis == dim else 1 for axis in range(len(dims))])
    return gain


def gaussian(stream_key, dims, scale, most, split=(), kind=jnp.bfloat16):
    values = jax.random.normal(stream_key, dims, jnp.float32) * scale
    if len(split) > 0:
        values = shard_levels(stream_key, dims, split, -0.22, 0.18) * values
    return jnp.clip(values, min=-most, max=most).astype(kind)


def setup_inputs(seed: int = 0) -> dict:
    key_list = jax.random.split(jax.random.key(seed), 6)
    return {
        "start_states": gaussian(key_list[0], (WINDOWS, 3, NROWS, COLS), 0.3, 1.5, ((0, 16), (2, 2)), jnp.float32),
        "obs_cells": place_ends(jax.random.randint(key_list[1], (WINDOWS, STEPS, OBS * N_STRIP), 0, ROWS_DEV * COLS), jax.random.fold_in(key_list[1], 1), 0, (ROWS_DEV * COLS) - 1).astype(jnp.int32),
        "obs_values": gaussian(key_list[2], (WINDOWS, STEPS, OBS * N_STRIP), 0.3, 1.5, ((0, 16), (2, 2)), jnp.float32),
        "weighting": gaussian(key_list[3], (3, BLOCK, BLOCK), BLOCK ** -0.5, 0.5, (), jnp.float32),
        "live_windows": place_ends((jax.random.randint(key_list[4], (WINDOWS,), 0, 4) < 3).astype(jnp.int32), jax.random.fold_in(key_list[4], 1), 0, 1),
    }


TIME_STEP = 0.2
DIFFUSION = 0.12
CORIOLIS = 0.5
STEP_LENGTH = 0.5

def col_diff(field):
    return (jnp.roll(field[1:-1], -1, 1) - jnp.roll(field[1:-1], 1, 1)) * 0.5

def row_diff(field):
    return (field[2:] - field[:-2]) * 0.5

def laplace(field):
    inner = field[1:-1]
    return field[2:] + field[:-2] + jnp.roll(inner, -1, 1) + jnp.roll(inner, 1, 1) - 4.0 * inner

def advance(padded):
    height, east_wind, north_wind = (padded[0], padded[1], padded[2])
    depth = 1.0 + height
    flux_east = east_wind * depth
    flux_north = north_wind * depth
    height_in, east_in, north_in = (height[1:-1], east_wind[1:-1], north_wind[1:-1])
    new_height = height_in - TIME_STEP * (col_diff(flux_east) + row_diff(flux_north)) + DIFFUSION * laplace(height)
    new_east = east_in - TIME_STEP * (col_diff(height) + east_in * col_diff(east_wind) + north_in * row_diff(east_wind)) + TIME_STEP * CORIOLIS * north_in + DIFFUSION * laplace(east_wind)
    new_north = north_in - TIME_STEP * (row_diff(height) + east_in * col_diff(north_wind) + north_in * row_diff(north_wind)) - TIME_STEP * CORIOLIS * east_in + DIFFUSION * laplace(north_wind)
    return jnp.stack([new_height, new_east, new_north])

def advance_whole(state):
    return advance(jnp.pad(state, ((0, 0), (1, 1), (0, 0))))

def weigh(defect, weighting):
    fields, rows, cols = defect.shape
    width = weighting.shape[1]
    blocks = defect.reshape(fields, rows, cols // width, width)
    mixed = jnp.einsum('frbi,fij->frbj', blocks, weighting, precision=lax.Precision.HIGHEST)
    return defect + mixed.reshape(fields, rows, cols)

def forcing(adjoint, state, cells, values, alive):
    rows, cols = (state.shape[1], state.shape[2])
    flat = state[0].reshape(rows * cols)
    innovation = (flat[cells] - values) * alive
    added = jnp.zeros((rows * cols,), state.dtype).at[cells].add(innovation)
    return adjoint.at[0].add(added.reshape(rows, cols))

def reference(start_states, obs_cells, obs_values, weighting, live_windows):
    strip_of = (jnp.arange(obs_cells.shape[2]) // OBS).astype(jnp.int32)
    offsets = (strip_of * (ROWS_DEV * COLS)).astype(jnp.int32)

    def run(state):
        for moment in range(STEPS):
            state = advance_whole(state)
        return state
    ends = lax.map(run, start_states)
    previous = jnp.concatenate([jnp.zeros_like(ends[:1]), ends[:-1]], 0)
    weighted = lax.map(lambda defect: weigh(defect, weighting), start_states - previous)
    following = jnp.concatenate([weighted[1:], jnp.zeros_like(weighted[:1])], 0)
    live = live_windows.astype(start_states.dtype)

    def adjoint_window(items):
        state, cells, values, alive, successor = items
        cells = (cells + offsets[None, :]).astype(jnp.int32)
        trajectory = [state]
        for moment in range(STEPS):
            trajectory.append(advance_whole(trajectory[-1]))
        adjoint = forcing(-successor, trajectory[STEPS], cells[STEPS - 1], values[STEPS - 1], alive)
        for moment in range(STEPS - 1, -1, -1):
            unused, pullback = jax.vjp(advance_whole, trajectory[moment])
            adjoint = pullback(adjoint)[0]
            if moment > 0:
                adjoint = forcing(adjoint, trajectory[moment], cells[moment - 1], values[moment - 1], alive)
        return adjoint
    adjoints = lax.map(adjoint_window, (start_states, obs_cells, obs_values, live, following))
    gradient = weighted + adjoints
    return (gradient, start_states - STEP_LENGTH * gradient)
```

```python
import functools

import jax
import jax.numpy as jnp
from jax import lax
from jax.experimental import pallas as pl
from jax.experimental.pallas import tpu as pltpu
from jax.sharding import PartitionSpec as P

TIME_STEP = 0.2
DIFFUSION = 0.12
CORIOLIS = 0.5
STEP_LENGTH = 0.5
LANES = 128
SUBS = 8
CHUNK = 2


def next_col(x, last_lane):
    turned = pltpu.roll(x, LANES - 1, 2)
    return jnp.where(last_lane, pltpu.roll(turned, SUBS - 1, 1), turned)


def prev_col(x, first_lane):
    turned = pltpu.roll(x, 1, 2)
    return jnp.where(first_lane, pltpu.roll(turned, 1, 1), turned)


def kernel(
    n_win, n_strip,
    start_hbm, cells_hbm, values_hbm, weight_hbm, live_hbm,
    grad_hbm, ana_hbm,
    own, above, below, nxt, prev_end, cells, values, weight, live,
    rhs, traj, saved, end, lam, counts, sums, nw, spill_up, spill_down, got_top, got_bot,
    grad, ana,
    local_sem, out_sem, send_sem, recv_sem,
):
    fields, rows, cols = own.shape
    steps = cells.shape[0]
    span = rows + 2 * steps
    pad = 1
    win, strip = lax.axis_index("win"), lax.axis_index("strip")
    has_prev, has_next = win > 0, win < n_win - 1
    has_up, has_down = strip > 0, strip < n_strip - 1

    def at_win(by):
        return {"win": jnp.clip(win + by, 0, n_win - 1)}

    def at_strip(by):
        return {"strip": jnp.clip(strip + by, 0, n_strip - 1)}

    loads = [
        pltpu.make_async_copy(start_hbm.at[0], own, local_sem.at[0]),
        pltpu.make_async_copy(cells_hbm.at[0], cells, local_sem.at[1]),
        pltpu.make_async_copy(values_hbm.at[0], values, local_sem.at[2]),
        pltpu.make_async_copy(weight_hbm, weight, local_sem.at[3]),
        pltpu.make_async_copy(live_hbm, live, local_sem.at[4]),
    ]
    for load in loads:
        load.start()

    barrier = pltpu.get_barrier_semaphore()
    for there, peer in ((has_up, at_strip(-1)), (has_down, at_strip(1)), (has_prev, at_win(-1)), (has_next, at_win(1))):
        @pl.when(there)
        def _():
            pl.semaphore_signal(barrier, inc=1, device_id=peer, device_id_type=pl.DeviceIdType.MESH)
    pl.semaphore_wait(barrier, sum(there.astype(jnp.int32) for there in (has_up, has_down, has_prev, has_next)))

    def remote(src, dst, sem, peer):
        return pltpu.make_async_remote_copy(
            src_ref=src, dst_ref=dst, send_sem=send_sem.at[sem], recv_sem=recv_sem.at[sem],
            device_id=peer, device_id_type=pl.DeviceIdType.MESH,
        )

    halo_up = remote(start_hbm.at[0, :, 0:SUBS, :], below, 0, at_strip(-1))
    halo_down = remote(start_hbm.at[0, :, rows - SUBS:rows, :], above, 1, at_strip(1))
    start_back = [remote(start_hbm.at[0, f], nxt.at[f], 2 + f, at_win(-1)) for f in range(fields)]
    end_on = remote(end, prev_end, 5, at_win(1))
    spill_to_up = remote(spill_up, got_bot, 6, at_strip(-1))
    spill_to_down = remote(spill_down, got_top, 7, at_strip(1))

    @pl.when(has_up)
    def _():
        halo_up.start()

    @pl.when(has_down)
    def _():
        halo_down.start()

    @pl.when(has_prev)
    def _():
        for copy in start_back:
            copy.start()

    lane = lax.broadcasted_iota(jnp.int32, (1, SUBS, LANES), 2)
    first_lane, last_lane = lane == 0, lane == LANES - 1
    zero_row = jnp.zeros((SUBS, LANES), jnp.float32)

    for buf in range(2):
        for f in range(fields):
            for row in list(range(0, steps + pad)) + list(range(steps + pad + rows, span + 2 * pad)):
                lam[buf, f, SUBS * row:SUBS * (row + 1), :] = zero_row
    for j in range(steps):
        for row in (j - 1 + pad, span - j + pad):
            for f in range(fields):
                traj[j, f, SUBS * row:SUBS * (row + 1), :] = zero_row
        for row in (j + pad, span - j - 1 + pad):
            for f in range(fields):
                saved[j, f, SUBS * row:SUBS * (row + 1), :] = zero_row

    loads[0].wait()
    for f in range(fields):
        for g in range(0, rows, SUBS):
            for b in range(SUBS):
                base = SUBS * (steps + pad + g) + b
                traj[0, f, pl.ds(base, SUBS, stride=SUBS), :] = own[f, g:g + SUBS, b * LANES:(b + 1) * LANES]

    loads[1].wait()
    loads[2].wait()
    loads[4].wait()
    alive = live[0].astype(jnp.float32)
    n_obs = cells.shape[1]
    tiles = rows * SUBS
    tile_id = lax.broadcasted_iota(jnp.int32, (tiles, n_obs), 0)
    lane_id = lax.broadcasted_iota(jnp.int32, (LANES, n_obs), 0)
    for j in range(steps):
        cell = cells[j:j + 1, :]
        value = values[j:j + 1, :]
        in_tile = tile_id == lax.shift_right_logical(cell, 7)
        in_lane = lane_id == (cell & (LANES - 1))
        high = value.astype(jnp.bfloat16).astype(jnp.float32)
        low = value - high
        picks = jnp.concatenate(
            [
                jnp.where(in_tile, 1.0, 0.0).astype(jnp.bfloat16),
                jnp.where(in_tile, high, 0.0).astype(jnp.bfloat16),
                jnp.where(in_tile, low, 0.0).astype(jnp.bfloat16),
            ],
            axis=0,
        )
        dense = lax.dot_general(
            picks, jnp.where(in_lane, 1.0, 0.0).astype(jnp.bfloat16),
            (((1,), (1,)), ((), ())), preferred_element_type=jnp.float32,
        )
        counts[j] = alive * dense[:tiles]
        sums[j] = alive * (dense[tiles:2 * tiles] + dense[2 * tiles:])

    loads[3].wait()
    for f in range(fields):
        w = weight[f]
        w_high = w.astype(jnp.bfloat16)
        w_low = (w - w_high.astype(jnp.float32)).astype(jnp.bfloat16)
        rhs[f, 0:LANES, 0:LANES] = w_high
        rhs[f, 0:LANES, LANES:] = w_low
        rhs[f, LANES:, 0:LANES] = w_high
        rhs[f, LANES:, LANES:] = jnp.zeros_like(w_low)

    def weigh(f, defect):
        high = defect.astype(jnp.bfloat16)
        low = (defect - high.astype(jnp.float32)).astype(jnp.bfloat16)
        out = jnp.dot(jnp.concatenate([high, low], axis=1), rhs[f], preferred_element_type=jnp.float32)
        return defect + (out[:, :LANES] + out[:, LANES:])

    for there, copy, src, src_row, dst_row in (
        (has_up, halo_down, above, SUBS - steps, pad),
        (has_down, halo_up, below, 0, pad + steps + rows),
    ):
        @pl.when(there)
        def _():
            copy.wait_recv()
            for f in range(fields):
                for b in range(SUBS):
                    base = SUBS * dst_row + b
                    traj[0, f, pl.ds(base, steps, stride=SUBS), :] = src[f, src_row:src_row + steps, b * LANES:(b + 1) * LANES]

        @pl.when(jnp.logical_not(there))
        def _():
            for f in range(fields):
                traj[0, f, SUBS * dst_row:SUBS * (dst_row + steps), :] = jnp.zeros((SUBS * steps, LANES), jnp.float32)

    up_mask = jnp.where(has_up, 1.0, 0.0).astype(jnp.float32)
    down_mask = jnp.where(has_down, 1.0, 0.0).astype(jnp.float32)

    def pieces(lo, hi):
        edges = []
        for a, b, mask in ((lo, min(hi, steps), up_mask), (steps + rows, hi, down_mask), (steps, steps + rows, None)):
            for r in range(a, b, CHUNK):
                edges.append((r, min(r + CHUNK, b), mask))
        return edges

    def tiles_of(ref, index, lo, hi):
        return ref[index + (slice(SUBS * (lo + pad), SUBS * (hi + pad)), slice(None))].reshape(hi - lo, SUBS, LANES)

    def put(ref, index, lo, value):
        count = value.shape[0]
        ref[index + (slice(SUBS * (lo + pad), SUBS * (lo + count + pad)), slice(None))] = value.reshape(count * SUBS, LANES)

    half = 0.5 * TIME_STEP
    turn = TIME_STEP * CORIOLIS

    for j in range(steps):
        for lo, hi, mask in pieces(j + 1, span - j - 1):
            h = tiles_of(traj, (j, 0), lo - 1, hi + 1)
            e = tiles_of(traj, (j, 1), lo - 1, hi + 1)
            n = tiles_of(traj, (j, 2), lo - 1, hi + 1)
            h0, e0, n0 = h[1:-1], e[1:-1], n[1:-1]
            hr, er, nr = (next_col(x, last_lane) for x in (h0, e0, n0))
            hl, el, nl = (prev_col(x, first_lane) for x in (h0, e0, n0))
            n_dx = nr - nl
            put(saved, (j, 0), lo, el)
            put(saved, (j, 1), lo, er)
            put(saved, (j, 2), lo, n_dx)
            flux_n = n * h + n
            he = h0 * (1.0 - 4.0 * DIFFUSION) - half * ((er * hr + er) - (el * hl + el) + flux_n[2:] - flux_n[:-2]) + DIFFUSION * (hr + hl + h[2:] + h[:-2])
            ee = e0 * (1.0 - 4.0 * DIFFUSION) - half * ((hr - hl) + e0 * (er - el) + n0 * (e[2:] - e[:-2])) + turn * n0 + DIFFUSION * (er + el + e[2:] + e[:-2])
            ne = n0 * (1.0 - 4.0 * DIFFUSION) - half * ((h[2:] - h[:-2]) + e0 * n_dx + n0 * (n[2:] - n[:-2])) - turn * e0 + DIFFUSION * (nr + nl + n[2:] + n[:-2])
            for f, x in enumerate((he, ee, ne)):
                if mask is not None:
                    x = x * mask
                if j + 1 < steps:
                    put(traj, (j + 1, f), lo, x)
                else:
                    put(end, (f,), lo - steps - pad, x)

    @pl.when(has_next)
    def _():
        end_on.start()

    for f in range(fields):
        @pl.when(has_next)
        def _():
            start_back[f].wait_recv()
            for g in range(0, rows, SUBS):
                for b in range(SUBS):
                    nw[f, pl.ds(SUBS * g + b, SUBS, stride=SUBS), :] = nxt[f, g:g + SUBS, b * LANES:(b + 1) * LANES]
            nw[f] = weigh(f, nw[f] - end[f])

        @pl.when(jnp.logical_not(has_next))
        def _():
            nw[f] = jnp.zeros((tiles, LANES), jnp.float32)

    own_rows = slice(SUBS * (steps + pad), SUBS * (steps + rows + pad))
    for f in range(fields):
        force = -nw[f]
        if f == 0:
            force = force + (counts[steps - 1] * end[0] - sums[steps - 1])
        lam[0, f, own_rows, :] = force

    for j in range(steps - 1, -1, -1):
        now = (steps - 1 - j) % 2
        later = 1 - now
        for lo, hi, mask in pieces(j, span - j):
            p, q, r = (tiles_of(lam, (now, f), lo - 1, hi + 1) for f in range(3))
            h0 = tiles_of(traj, (j, 0), lo, hi)
            e = tiles_of(traj, (j, 1), lo - 1, hi + 1)
            n = tiles_of(traj, (j, 2), lo - 1, hi + 1)
            el = tiles_of(saved, (j, 0), lo, hi)
            er = tiles_of(saved, (j, 1), lo, hi)
            n_dx = tiles_of(saved, (j, 2), lo, hi)
            e0, n0 = e[1:-1], n[1:-1]
            p0, q0, r0 = p[1:-1], q[1:-1], r[1:-1]
            pr, qr, rr = (next_col(x, last_lane) for x in (p0, q0, r0))
            pl_, ql, rl = (prev_col(x, first_lane) for x in (p0, q0, r0))
            dxp, dyp = pr - pl_, p[2:] - p[:-2]
            qn, rn = q * n, r * n
            ah = p0 * (1.0 - 4.0 * DIFFUSION) + half * (e0 * dxp + n0 * dyp + (qr - ql) + (r[2:] - r[:-2])) + DIFFUSION * (pr + pl_ + p[2:] + p[:-2])
            ae = q0 * (1.0 - 4.0 * DIFFUSION) + half * ((h0 * dxp + dxp) - q0 * (er - el) + (qr * er - ql * el) + (qn[2:] - qn[:-2]) - r0 * n_dx) - turn * r0 + DIFFUSION * (qr + ql + q[2:] + q[:-2])
            an = r0 * (1.0 - 4.0 * DIFFUSION) + half * ((h0 * dyp + dyp) - q0 * (e[2:] - e[:-2]) - r0 * (n[2:] - n[:-2]) + (rr * er - rl * el) + (rn[2:] - rn[:-2])) + turn * q0 + DIFFUSION * (rr + rl + r[2:] + r[:-2])
            if j > 0 and mask is None:
                at = slice(SUBS * (lo - steps), SUBS * (hi - steps))
                shape = (hi - lo, SUBS, LANES)
                ah = ah + (counts[j - 1, at, :].reshape(shape) * h0 - sums[j - 1, at, :].reshape(shape))
            for f, x in enumerate((ah, ae, an)):
                if mask is not None:
                    x = x * mask
                if j == 0 and lo < steps:
                    spill_up[f, SUBS * lo:SUBS * hi, :] = x.reshape((hi - lo) * SUBS, LANES)
                elif j == 0 and lo >= steps + rows:
                    at = slice(SUBS * (lo - steps - rows), SUBS * (hi - steps - rows))
                    spill_down[f, at, :] = x.reshape((hi - lo) * SUBS, LANES)
                else:
                    put(lam, (later, f), lo, x)
            if j == 0 and hi == span:
                @pl.when(has_up)
                def _():
                    spill_to_up.start()

                @pl.when(has_down)
                def _():
                    spill_to_down.start()

    last = steps % 2

    @pl.when(has_prev)
    def _():
        end_on.wait_recv()

    @pl.when(jnp.logical_not(has_prev))
    def _():
        prev_end[...] = jnp.zeros_like(prev_end)

    for f in range(fields):
        start = traj[0, f, own_rows, :]
        lam[last, f, own_rows, :] = lam[last, f, own_rows, :] + weigh(f, start - prev_end[f])

    @pl.when(has_up)
    def _():
        spill_to_down.wait_recv()
        for f in range(fields):
            at = slice(SUBS * (steps + pad), SUBS * (2 * steps + pad))
            lam[last, f, at, :] = lam[last, f, at, :] + got_top[f]

    @pl.when(has_down)
    def _():
        spill_to_up.wait_recv()
        for f in range(fields):
            at = slice(SUBS * (rows + pad), SUBS * (steps + rows + pad))
            lam[last, f, at, :] = lam[last, f, at, :] + got_bot[f]

    for f in range(fields):
        for g in range(0, rows, SUBS):
            for b in range(SUBS):
                at = pl.ds(SUBS * (steps + pad + g) + b, SUBS, stride=SUBS)
                value = lam[last, f, at, :]
                where = (f, slice(g, g + SUBS), slice(b * LANES, (b + 1) * LANES))
                grad[where] = value
                ana[where] = own[where] - STEP_LENGTH * value

    out = [
        pltpu.make_async_copy(grad, grad_hbm.at[0], out_sem.at[0]),
        pltpu.make_async_copy(ana, ana_hbm.at[0], out_sem.at[1]),
    ]
    for copy in out:
        copy.start()
    for there, copies in (
        (has_up, [halo_up, spill_to_up]),
        (has_down, [halo_down, spill_to_down]),
        (has_prev, start_back),
        (has_next, [end_on]),
    ):
        @pl.when(there)
        def _():
            for copy in copies:
                copy.wait_send()
    for copy in out:
        copy.wait()


def per_device(start_states, obs_cells, obs_values, weighting, live_windows):
    n_win, n_strip = lax.axis_size("win"), lax.axis_size("strip")
    _, fields, rows, cols = start_states.shape
    steps, n_obs = obs_cells.shape[1:]
    span = rows + 2 * steps + 2
    f32 = jnp.float32
    hbm = pl.BlockSpec(memory_space=pl.ANY)
    out = jax.ShapeDtypeStruct(start_states.shape, f32)
    dma = pltpu.SemaphoreType.DMA
    return pl.pallas_call(
        functools.partial(kernel, n_win, n_strip),
        out_shape=(out, out),
        in_specs=[hbm] * 5,
        out_specs=(hbm, hbm),
        scratch_shapes=[
            pltpu.VMEM((fields, rows, cols), f32),
            pltpu.VMEM((fields, SUBS, cols), f32),
            pltpu.VMEM((fields, SUBS, cols), f32),
            pltpu.VMEM((fields, rows, cols), f32),
            pltpu.VMEM((fields, rows * SUBS, LANES), f32),
            pltpu.VMEM((steps, n_obs), jnp.int32),
            pltpu.VMEM((steps, n_obs), f32),
            pltpu.VMEM(weighting.shape, f32),
            pltpu.SMEM((1,), jnp.int32),
            pltpu.VMEM((fields, 2 * LANES, 2 * LANES), jnp.bfloat16),
            pltpu.VMEM((steps, fields, span * SUBS, LANES), f32),
            pltpu.VMEM((steps, fields, span * SUBS, LANES), f32),
            pltpu.VMEM((fields, rows * SUBS, LANES), f32),
            pltpu.VMEM((2, fields, span * SUBS, LANES), f32),
            pltpu.VMEM((steps, rows * SUBS, LANES), f32),
            pltpu.VMEM((steps, rows * SUBS, LANES), f32),
            pltpu.VMEM((fields, rows * SUBS, LANES), f32),
            pltpu.VMEM((fields, steps * SUBS, LANES), f32),
            pltpu.VMEM((fields, steps * SUBS, LANES), f32),
            pltpu.VMEM((fields, steps * SUBS, LANES), f32),
            pltpu.VMEM((fields, steps * SUBS, LANES), f32),
            pltpu.VMEM((fields, rows, cols), f32),
            pltpu.VMEM((fields, rows, cols), f32),
            dma((5,)),
            dma((2,)),
            dma((8,)),
            dma((8,)),
        ],
        compiler_params=pltpu.CompilerParams(collective_id=0, has_side_effects=True),
    )(start_states, obs_cells, obs_values, weighting, live_windows)


def solution(mesh):
    placed = (
        P("win", None, "strip", None),
        P("win", None, "strip"),
        P("win", None, "strip"),
        P(),
        P("win"),
    )
    return jax.shard_map(
        per_device,
        mesh=mesh,
        in_specs=placed,
        out_specs=(P("win", None, "strip", None), P("win", None, "strip", None)),
        check_vma=False,
    )
```

```python
import functools

import jax
import jax.numpy as jnp
from jax import lax
from jax.experimental import pallas as pl
from jax.experimental.pallas import tpu as pltpu
from jax.sharding import PartitionSpec as P

TIME_STEP = 0.2
DIFFUSION = 0.12
CORIOLIS = 0.5
STEP_LENGTH = 0.5
LANES = 128
SUBS = 8
CHUNK = 2


def next_col(x, last_lane):
    turned = pltpu.roll(x, LANES - 1, 2)
    return jnp.where(last_lane, pltpu.roll(turned, SUBS - 1, 1), turned)


def prev_col(x, first_lane):
    turned = pltpu.roll(x, 1, 2)
    return jnp.where(first_lane, pltpu.roll(turned, 1, 1), turned)


def kernel(
    n_win, n_strip,
    start_hbm, cells_hbm, values_hbm, weight_hbm, live_hbm,
    grad,
    own, above, below, nxt, prev_end, cells, values, weight, live,
    rhs, traj, saved, end, lam, counts, sums, nw, spill_up, spill_down, got_top, got_bot,
    local_sem, send_sem, recv_sem,
):
    fields, rows, cols = own.shape
    steps = cells.shape[0]
    span = rows + 2 * steps
    pad = 1
    win, strip = lax.axis_index("win"), lax.axis_index("strip")
    has_prev, has_next = win > 0, win < n_win - 1
    has_up, has_down = strip > 0, strip < n_strip - 1

    def at_win(by):
        return {"win": jnp.clip(win + by, 0, n_win - 1)}

    def at_strip(by):
        return {"strip": jnp.clip(strip + by, 0, n_strip - 1)}

    loads = [
        pltpu.make_async_copy(start_hbm.at[0], own, local_sem.at[0]),
        pltpu.make_async_copy(cells_hbm.at[0], cells, local_sem.at[1]),
        pltpu.make_async_copy(values_hbm.at[0], values, local_sem.at[2]),
        pltpu.make_async_copy(weight_hbm, weight, local_sem.at[3]),
        pltpu.make_async_copy(live_hbm, live, local_sem.at[4]),
    ]
    for load in loads:
        load.start()

    barrier = pltpu.get_barrier_semaphore()
    for there, peer in ((has_up, at_strip(-1)), (has_down, at_strip(1)), (has_prev, at_win(-1)), (has_next, at_win(1))):
        @pl.when(there)
        def _():
            pl.semaphore_signal(barrier, inc=1, device_id=peer, device_id_type=pl.DeviceIdType.MESH)
    pl.semaphore_wait(barrier, sum(there.astype(jnp.int32) for there in (has_up, has_down, has_prev, has_next)))

    def remote(src, dst, sem, peer):
        return pltpu.make_async_remote_copy(
            src_ref=src, dst_ref=dst, send_sem=send_sem.at[sem], recv_sem=recv_sem.at[sem],
            device_id=peer, device_id_type=pl.DeviceIdType.MESH,
        )

    halo_up = remote(start_hbm.at[0, :, 0:SUBS, :], below, 0, at_strip(-1))
    halo_down = remote(start_hbm.at[0, :, rows - SUBS:rows, :], above, 1, at_strip(1))
    start_back = [remote(start_hbm.at[0, f], nxt.at[f], 2 + f, at_win(-1)) for f in range(fields)]
    end_on = remote(end, prev_end, 5, at_win(1))
    spill_to_up = remote(spill_up, got_bot, 6, at_strip(-1))
    spill_to_down = remote(spill_down, got_top, 7, at_strip(1))

    @pl.when(has_up)
    def _():
        halo_up.start()

    @pl.when(has_down)
    def _():
        halo_down.start()

    @pl.when(has_prev)
    def _():
        for copy in start_back:
            copy.start()

    lane = lax.broadcasted_iota(jnp.int32, (1, SUBS, LANES), 2)
    first_lane, last_lane = lane == 0, lane == LANES - 1
    zero_row = jnp.zeros((SUBS, LANES), jnp.float32)

    for buf in range(2):
        for f in range(fields):
            for row in list(range(0, steps + pad)) + list(range(steps + pad + rows, span + 2 * pad)):
                lam[buf, f, SUBS * row:SUBS * (row + 1), :] = zero_row
    for j in range(steps):
        for row in (j - 1 + pad, span - j + pad):
            for f in range(fields):
                traj[j, f, SUBS * row:SUBS * (row + 1), :] = zero_row
        for row in (j + pad, span - j - 1 + pad):
            for f in range(fields):
                saved[j, f, SUBS * row:SUBS * (row + 1), :] = zero_row

    loads[0].wait()
    for f in range(fields):
        for g in range(0, rows, SUBS):
            for b in range(SUBS):
                base = SUBS * (steps + pad + g) + b
                traj[0, f, pl.ds(base, SUBS, stride=SUBS), :] = own[f, g:g + SUBS, b * LANES:(b + 1) * LANES]

    loads[1].wait()
    loads[2].wait()
    loads[4].wait()
    alive = live[0].astype(jnp.float32)
    n_obs = cells.shape[1]
    tiles = rows * SUBS
    tile_id = lax.broadcasted_iota(jnp.int32, (tiles, n_obs), 0)
    lane_id = lax.broadcasted_iota(jnp.int32, (LANES, n_obs), 0)
    for j in range(steps):
        cell = cells[j:j + 1, :]
        value = values[j:j + 1, :]
        in_tile = tile_id == lax.shift_right_logical(cell, 7)
        in_lane = lane_id == (cell & (LANES - 1))
        high = value.astype(jnp.bfloat16).astype(jnp.float32)
        low = value - high
        picks = jnp.concatenate(
            [
                jnp.where(in_tile, 1.0, 0.0).astype(jnp.bfloat16),
                jnp.where(in_tile, high, 0.0).astype(jnp.bfloat16),
                jnp.where(in_tile, low, 0.0).astype(jnp.bfloat16),
            ],
            axis=0,
        )
        dense = lax.dot_general(
            picks, jnp.where(in_lane, 1.0, 0.0).astype(jnp.bfloat16),
            (((1,), (1,)), ((), ())), preferred_element_type=jnp.float32,
        )
        counts[j] = alive * dense[:tiles]
        sums[j] = alive * (dense[tiles:2 * tiles] + dense[2 * tiles:])

    loads[3].wait()
    for f in range(fields):
        w = weight[f]
        w_high = w.astype(jnp.bfloat16)
        w_low = (w - w_high.astype(jnp.float32)).astype(jnp.bfloat16)
        rhs[f, 0:LANES, 0:LANES] = w_high
        rhs[f, 0:LANES, LANES:] = w_low
        rhs[f, LANES:, 0:LANES] = w_high
        rhs[f, LANES:, LANES:] = jnp.zeros_like(w_low)

    def weigh(f, defect):
        high = defect.astype(jnp.bfloat16)
        low = (defect - high.astype(jnp.float32)).astype(jnp.bfloat16)
        out = jnp.dot(jnp.concatenate([high, low], axis=1), rhs[f], preferred_element_type=jnp.float32)
        return defect + (out[:, :LANES] + out[:, LANES:])

    for there, copy, src, src_row, dst_row in (
        (has_up, halo_down, above, SUBS - steps, pad),
        (has_down, halo_up, below, 0, pad + steps + rows),
    ):
        @pl.when(there)
        def _():
            copy.wait_recv()
            for f in range(fields):
                for b in range(SUBS):
                    base = SUBS * dst_row + b
                    traj[0, f, pl.ds(base, steps, stride=SUBS), :] = src[f, src_row:src_row + steps, b * LANES:(b + 1) * LANES]

        @pl.when(jnp.logical_not(there))
        def _():
            for f in range(fields):
                traj[0, f, SUBS * dst_row:SUBS * (dst_row + steps), :] = jnp.zeros((SUBS * steps, LANES), jnp.float32)

    up_mask = jnp.where(has_up, 1.0, 0.0).astype(jnp.float32)
    down_mask = jnp.where(has_down, 1.0, 0.0).astype(jnp.float32)

    def pieces(lo, hi):
        edges = []
        for a, b, mask in ((lo, min(hi, steps), up_mask), (steps + rows, hi, down_mask), (steps, steps + rows, None)):
            for r in range(a, b, CHUNK):
                edges.append((r, min(r + CHUNK, b), mask))
        return edges

    def tiles_of(ref, index, lo, hi):
        return ref[index + (slice(SUBS * (lo + pad), SUBS * (hi + pad)), slice(None))].reshape(hi - lo, SUBS, LANES)

    def put(ref, index, lo, value):
        count = value.shape[0]
        ref[index + (slice(SUBS * (lo + pad), SUBS * (lo + count + pad)), slice(None))] = value.reshape(count * SUBS, LANES)

    half = 0.5 * TIME_STEP
    turn = TIME_STEP * CORIOLIS

    for j in range(steps):
        for lo, hi, mask in pieces(j + 1, span - j - 1):
            h = tiles_of(traj, (j, 0), lo - 1, hi + 1)
            e = tiles_of(traj, (j, 1), lo - 1, hi + 1)
            n = tiles_of(traj, (j, 2), lo - 1, hi + 1)
            h0, e0, n0 = h[1:-1], e[1:-1], n[1:-1]
            hr, er, nr = (next_col(x, last_lane) for x in (h0, e0, n0))
            hl, el, nl = (prev_col(x, first_lane) for x in (h0, e0, n0))
            n_dx = nr - nl
            put(saved, (j, 0), lo, el)
            put(saved, (j, 1), lo, er)
            put(saved, (j, 2), lo, n_dx)
            flux_n = n * h + n
            he = h0 * (1.0 - 4.0 * DIFFUSION) - half * ((er * hr + er) - (el * hl + el) + flux_n[2:] - flux_n[:-2]) + DIFFUSION * (hr + hl + h[2:] + h[:-2])
            ee = e0 * (1.0 - 4.0 * DIFFUSION) - half * ((hr - hl) + e0 * (er - el) + n0 * (e[2:] - e[:-2])) + turn * n0 + DIFFUSION * (er + el + e[2:] + e[:-2])
            ne = n0 * (1.0 - 4.0 * DIFFUSION) - half * ((h[2:] - h[:-2]) + e0 * n_dx + n0 * (n[2:] - n[:-2])) - turn * e0 + DIFFUSION * (nr + nl + n[2:] + n[:-2])
            for f, x in enumerate((he, ee, ne)):
                if mask is not None:
                    x = x * mask
                if j + 1 < steps:
                    put(traj, (j + 1, f), lo, x)
                else:
                    put(end, (f,), lo - steps - pad, x)

    @pl.when(has_next)
    def _():
        end_on.start()

    for f in range(fields):
        @pl.when(has_next)
        def _():
            start_back[f].wait_recv()
            for g in range(0, rows, SUBS):
                for b in range(SUBS):
                    nw[f, pl.ds(SUBS * g + b, SUBS, stride=SUBS), :] = nxt[f, g:g + SUBS, b * LANES:(b + 1) * LANES]
            nw[f] = weigh(f, nw[f] - end[f])

        @pl.when(jnp.logical_not(has_next))
        def _():
            nw[f] = jnp.zeros((tiles, LANES), jnp.float32)

    own_rows = slice(SUBS * (steps + pad), SUBS * (steps + rows + pad))
    for f in range(fields):
        force = -nw[f]
        if f == 0:
            force = force + (counts[steps - 1] * end[0] - sums[steps - 1])
        lam[0, f, own_rows, :] = force

    for j in range(steps - 1, -1, -1):
        now = (steps - 1 - j) % 2
        later = 1 - now
        for lo, hi, mask in pieces(j, span - j):
            p, q, r = (tiles_of(lam, (now, f), lo - 1, hi + 1) for f in range(3))
            h0 = tiles_of(traj, (j, 0), lo, hi)
            e = tiles_of(traj, (j, 1), lo - 1, hi + 1)
            n = tiles_of(traj, (j, 2), lo - 1, hi + 1)
            el = tiles_of(saved, (j, 0), lo, hi)
            er = tiles_of(saved, (j, 1), lo, hi)
            n_dx = tiles_of(saved, (j, 2), lo, hi)
            e0, n0 = e[1:-1], n[1:-1]
            p0, q0, r0 = p[1:-1], q[1:-1], r[1:-1]
            pr, qr, rr = (next_col(x, last_lane) for x in (p0, q0, r0))
            pl_, ql, rl = (prev_col(x, first_lane) for x in (p0, q0, r0))
            dxp, dyp = pr - pl_, p[2:] - p[:-2]
            qn, rn = q * n, r * n
            ah = p0 * (1.0 - 4.0 * DIFFUSION) + half * (e0 * dxp + n0 * dyp + (qr - ql) + (r[2:] - r[:-2])) + DIFFUSION * (pr + pl_ + p[2:] + p[:-2])
            ae = q0 * (1.0 - 4.0 * DIFFUSION) + half * ((h0 * dxp + dxp) - q0 * (er - el) + (qr * er - ql * el) + (qn[2:] - qn[:-2]) - r0 * n_dx) - turn * r0 + DIFFUSION * (qr + ql + q[2:] + q[:-2])
            an = r0 * (1.0 - 4.0 * DIFFUSION) + half * ((h0 * dyp + dyp) - q0 * (e[2:] - e[:-2]) - r0 * (n[2:] - n[:-2]) + (rr * er - rl * el) + (rn[2:] - rn[:-2])) + turn * q0 + DIFFUSION * (rr + rl + r[2:] + r[:-2])
            if j > 0 and mask is None:
                at = slice(SUBS * (lo - steps), SUBS * (hi - steps))
                shape = (hi - lo, SUBS, LANES)
                ah = ah + (counts[j - 1, at, :].reshape(shape) * h0 - sums[j - 1, at, :].reshape(shape))
            for f, x in enumerate((ah, ae, an)):
                if mask is not None:
                    x = x * mask
                if j == 0 and lo < steps:
                    spill_up[f, SUBS * lo:SUBS * hi, :] = x.reshape((hi - lo) * SUBS, LANES)
                elif j == 0 and lo >= steps + rows:
                    at = slice(SUBS * (lo - steps - rows), SUBS * (hi - steps - rows))
                    spill_down[f, at, :] = x.reshape((hi - lo) * SUBS, LANES)
                else:
                    put(lam, (later, f), lo, x)
            if j == 0 and hi == span:
                @pl.when(has_up)
                def _():
                    spill_to_up.start()

                @pl.when(has_down)
                def _():
                    spill_to_down.start()

    last = steps % 2

    @pl.when(has_prev)
    def _():
        end_on.wait_recv()

    @pl.when(jnp.logical_not(has_prev))
    def _():
        prev_end[...] = jnp.zeros_like(prev_end)

    for f in range(fields):
        start = traj[0, f, own_rows, :]
        grad[f] = lam[last, f, own_rows, :] + weigh(f, start - prev_end[f])

    @pl.when(has_up)
    def _():
        spill_to_down.wait_recv()
        for f in range(fields):
            at = slice(0, SUBS * steps)
            grad[f, at, :] = grad[f, at, :] + got_top[f]

    @pl.when(has_down)
    def _():
        spill_to_up.wait_recv()
        for f in range(fields):
            at = slice(SUBS * (rows - steps), SUBS * rows)
            grad[f, at, :] = grad[f, at, :] + got_bot[f]

    for there, copies in (
        (has_up, [halo_up, spill_to_up]),
        (has_down, [halo_down, spill_to_down]),
        (has_prev, start_back),
        (has_next, [end_on]),
    ):
        @pl.when(there)
        def _():
            for copy in copies:
                copy.wait_send()


def finish(tiled, start_hbm, grad_hbm, ana_hbm, own, grad, ana, sems):
    fields, rows, _ = own.shape
    load = pltpu.make_async_copy(start_hbm.at[0], own, sems.at[0])
    load.start()
    load.wait()
    out = []
    for f in range(fields):
        for g in range(0, rows, SUBS):
            for b in range(SUBS):
                value = tiled[f, pl.ds(SUBS * g + b, SUBS, stride=SUBS), :]
                where = (f, slice(g, g + SUBS), slice(b * LANES, (b + 1) * LANES))
                grad[where] = value
                ana[where] = own[where] - STEP_LENGTH * value
        out.append(pltpu.make_async_copy(grad.at[f], grad_hbm.at[0, f], sems.at[1 + 2 * f]))
        out.append(pltpu.make_async_copy(ana.at[f], ana_hbm.at[0, f], sems.at[2 + 2 * f]))
        out[-2].start()
        out[-1].start()
    for copy in out:
        copy.wait()


def per_device(start_states, obs_cells, obs_values, weighting, live_windows):
    n_win, n_strip = lax.axis_size("win"), lax.axis_size("strip")
    _, fields, rows, cols = start_states.shape
    steps, n_obs = obs_cells.shape[1:]
    span = rows + 2 * steps + 2
    f32 = jnp.float32
    hbm = pl.BlockSpec(memory_space=pl.ANY)
    out = jax.ShapeDtypeStruct(start_states.shape, f32)
    dma = pltpu.SemaphoreType.DMA
    gradient = pl.pallas_call(
        functools.partial(kernel, n_win, n_strip),
        out_shape=pltpu.VMEM((fields, rows * SUBS, LANES), f32),
        in_specs=[hbm] * 5,
        out_specs=pl.BlockSpec(memory_space=pltpu.VMEM),
        scratch_shapes=[
            pltpu.VMEM((fields, rows, cols), f32),
            pltpu.VMEM((fields, SUBS, cols), f32),
            pltpu.VMEM((fields, SUBS, cols), f32),
            pltpu.VMEM((fields, rows, cols), f32),
            pltpu.VMEM((fields, rows * SUBS, LANES), f32),
            pltpu.VMEM((steps, n_obs), jnp.int32),
            pltpu.VMEM((steps, n_obs), f32),
            pltpu.VMEM(weighting.shape, f32),
            pltpu.SMEM((1,), jnp.int32),
            pltpu.VMEM((fields, 2 * LANES, 2 * LANES), jnp.bfloat16),
            pltpu.VMEM((steps, fields, span * SUBS, LANES), f32),
            pltpu.VMEM((steps, fields, span * SUBS, LANES), f32),
            pltpu.VMEM((fields, rows * SUBS, LANES), f32),
            pltpu.VMEM((2, fields, span * SUBS, LANES), f32),
            pltpu.VMEM((steps, rows * SUBS, LANES), f32),
            pltpu.VMEM((steps, rows * SUBS, LANES), f32),
            pltpu.VMEM((fields, rows * SUBS, LANES), f32),
            pltpu.VMEM((fields, steps * SUBS, LANES), f32),
            pltpu.VMEM((fields, steps * SUBS, LANES), f32),
            pltpu.VMEM((fields, steps * SUBS, LANES), f32),
            pltpu.VMEM((fields, steps * SUBS, LANES), f32),
            dma((5,)),
            dma((8,)),
            dma((8,)),
        ],
        compiler_params=pltpu.CompilerParams(collective_id=0, has_side_effects=True),
    )(start_states, obs_cells, obs_values, weighting, live_windows)
    return pl.pallas_call(
        finish,
        out_shape=(out, out),
        in_specs=[pl.BlockSpec(memory_space=pltpu.VMEM), hbm],
        out_specs=(hbm, hbm),
        scratch_shapes=[pltpu.VMEM((fields, rows, cols), f32)] * 3 + [dma((1 + 2 * fields,))],
    )(pltpu.with_memory_space_constraint(gradient, pltpu.VMEM), start_states)


def solution(mesh):
    placed = (
        P("win", None, "strip", None),
        P("win", None, "strip"),
        P("win", None, "strip"),
        P(),
        P("win"),
    )
    return jax.shard_map(
        per_device,
        mesh=mesh,
        in_specs=placed,
        out_specs=(P("win", None, "strip", None), P("win", None, "strip", None)),
        check_vma=False,
    )
```

```python
import functools

import jax
import jax.numpy as jnp
from jax import lax
from jax.experimental import pallas as pl
from jax.experimental.pallas import tpu as pltpu
from jax.sharding import PartitionSpec as P

TIME_STEP = 0.2
DIFFUSION = 0.12
CORIOLIS = 0.5
STEP_LENGTH = 0.5
LANES = 128
SUBS = 8
CHUNK = 2


def next_col(x, last_lane):
    turned = pltpu.roll(x, LANES - 1, 2)
    return jnp.where(last_lane, pltpu.roll(turned, SUBS - 1, 1), turned)


def prev_col(x, first_lane):
    turned = pltpu.roll(x, 1, 2)
    return jnp.where(first_lane, pltpu.roll(turned, 1, 1), turned)


def kernel(
    n_win, n_strip,
    start_hbm, cells_hbm, values_hbm, weight_hbm, live_hbm,
    grad, own,
    above, below, nxt, prev_end, cells, values, weight, live,
    rhs, traj, saved, end, lam, counts, sums, nw, spill_up, spill_down, got_top, got_bot,
    local_sem, send_sem, recv_sem,
):
    fields, rows, cols = own.shape
    steps = cells.shape[0]
    span = rows + 2 * steps
    pad = 1
    win, strip = lax.axis_index("win"), lax.axis_index("strip")
    has_prev, has_next = win > 0, win < n_win - 1
    has_up, has_down = strip > 0, strip < n_strip - 1

    def at_win(by):
        return {"win": jnp.clip(win + by, 0, n_win - 1)}

    def at_strip(by):
        return {"strip": jnp.clip(strip + by, 0, n_strip - 1)}

    loads = [
        pltpu.make_async_copy(start_hbm.at[0], own, local_sem.at[0]),
        pltpu.make_async_copy(cells_hbm.at[0], cells, local_sem.at[1]),
        pltpu.make_async_copy(values_hbm.at[0], values, local_sem.at[2]),
        pltpu.make_async_copy(weight_hbm, weight, local_sem.at[3]),
        pltpu.make_async_copy(live_hbm, live, local_sem.at[4]),
    ]
    barrier = pltpu.get_barrier_semaphore()
    for there, peer in ((has_up, at_strip(-1)), (has_down, at_strip(1)), (has_prev, at_win(-1)), (has_next, at_win(1))):
        @pl.when(there)
        def _():
            pl.semaphore_signal(barrier, inc=1, device_id=peer, device_id_type=pl.DeviceIdType.MESH)
    for load in loads:
        load.start()

    pl.semaphore_wait(barrier, sum(there.astype(jnp.int32) for there in (has_up, has_down, has_prev, has_next)))

    def remote(src, dst, sem, peer):
        return pltpu.make_async_remote_copy(
            src_ref=src, dst_ref=dst, send_sem=send_sem.at[sem], recv_sem=recv_sem.at[sem],
            device_id=peer, device_id_type=pl.DeviceIdType.MESH,
        )

    halo_up = remote(start_hbm.at[0, :, 0:SUBS, :], below, 0, at_strip(-1))
    halo_down = remote(start_hbm.at[0, :, rows - SUBS:rows, :], above, 1, at_strip(1))
    start_back = [remote(start_hbm.at[0, f], nxt.at[f], 2 + f, at_win(-1)) for f in range(fields)]
    end_on = [remote(end.at[f], prev_end.at[f], 2 + fields + f, at_win(1)) for f in range(fields)]
    spill_to_up = remote(spill_up, got_bot, 2 + 2 * fields, at_strip(-1))
    spill_to_down = remote(spill_down, got_top, 3 + 2 * fields, at_strip(1))

    @pl.when(has_prev)
    def _():
        for copy in start_back:
            copy.start()

    @pl.when(has_up)
    def _():
        halo_up.start()

    @pl.when(has_down)
    def _():
        halo_down.start()

    lane = lax.broadcasted_iota(jnp.int32, (1, SUBS, LANES), 2)
    first_lane, last_lane = lane == 0, lane == LANES - 1
    zero_row = jnp.zeros((SUBS, LANES), jnp.float32)

    for buf in range(2):
        for f in range(fields):
            for row in list(range(0, steps + pad)) + list(range(steps + pad + rows, span + 2 * pad)):
                lam[buf, f, SUBS * row:SUBS * (row + 1), :] = zero_row
    for j in range(steps):
        for row in (j - 1 + pad, span - j + pad):
            for f in range(fields):
                traj[j, f, SUBS * row:SUBS * (row + 1), :] = zero_row
        for row in (j + pad, span - j - 1 + pad):
            for f in range(fields):
                saved[j, f, SUBS * row:SUBS * (row + 1), :] = zero_row

    loads[0].wait()
    for f in range(fields):
        for g in range(0, rows, SUBS):
            for b in range(SUBS):
                base = SUBS * (steps + pad + g) + b
                traj[0, f, pl.ds(base, SUBS, stride=SUBS), :] = own[f, g:g + SUBS, b * LANES:(b + 1) * LANES]

    loads[1].wait()
    loads[2].wait()
    loads[4].wait()
    alive = live[0].astype(jnp.float32)
    n_obs = cells.shape[1]
    tiles = rows * SUBS
    tile_id = lax.broadcasted_iota(jnp.int32, (tiles, n_obs), 0)
    lane_id = lax.broadcasted_iota(jnp.int32, (LANES, n_obs), 0)
    for j in range(steps):
        cell = cells[j:j + 1, :]
        value = values[j:j + 1, :]
        in_tile = tile_id == lax.shift_right_logical(cell, 7)
        in_lane = lane_id == (cell & (LANES - 1))
        high = value.astype(jnp.bfloat16).astype(jnp.float32)
        low = value - high
        picks = jnp.concatenate(
            [
                jnp.where(in_tile, 1.0, 0.0).astype(jnp.bfloat16),
                jnp.where(in_tile, high, 0.0).astype(jnp.bfloat16),
                jnp.where(in_tile, low, 0.0).astype(jnp.bfloat16),
            ],
            axis=0,
        )
        dense = lax.dot_general(
            picks, jnp.where(in_lane, 1.0, 0.0).astype(jnp.bfloat16),
            (((1,), (1,)), ((), ())), preferred_element_type=jnp.float32,
        )
        counts[j] = alive * dense[:tiles]
        sums[j] = alive * (dense[tiles:2 * tiles] + dense[2 * tiles:])

    loads[3].wait()
    for f in range(fields):
        w = weight[f]
        w_high = w.astype(jnp.bfloat16)
        w_low = (w - w_high.astype(jnp.float32)).astype(jnp.bfloat16)
        rhs[f, 0:LANES, 0:LANES] = w_high
        rhs[f, 0:LANES, LANES:] = w_low
        rhs[f, LANES:, 0:LANES] = w_high
        rhs[f, LANES:, LANES:] = jnp.zeros_like(w_low)

    def weigh(f, defect):
        high = defect.astype(jnp.bfloat16)
        low = (defect - high.astype(jnp.float32)).astype(jnp.bfloat16)
        out = jnp.dot(jnp.concatenate([high, low], axis=1), rhs[f], preferred_element_type=jnp.float32)
        return defect + (out[:, :LANES] + out[:, LANES:])

    for there, copy, src, src_row, dst_row in (
        (has_up, halo_down, above, SUBS - steps, pad),
        (has_down, halo_up, below, 0, pad + steps + rows),
    ):
        @pl.when(there)
        def _():
            copy.wait_recv()
            for f in range(fields):
                for b in range(SUBS):
                    base = SUBS * dst_row + b
                    traj[0, f, pl.ds(base, steps, stride=SUBS), :] = src[f, src_row:src_row + steps, b * LANES:(b + 1) * LANES]

        @pl.when(jnp.logical_not(there))
        def _():
            for f in range(fields):
                traj[0, f, SUBS * dst_row:SUBS * (dst_row + steps), :] = jnp.zeros((SUBS * steps, LANES), jnp.float32)

    up_mask = jnp.where(has_up, 1.0, 0.0).astype(jnp.float32)
    down_mask = jnp.where(has_down, 1.0, 0.0).astype(jnp.float32)

    def pieces(lo, hi):
        edges = []
        for a, b, mask in ((lo, min(hi, steps), up_mask), (steps + rows, hi, down_mask), (steps, steps + rows, None)):
            for r in range(a, b, CHUNK):
                edges.append((r, min(r + CHUNK, b), mask))
        return edges

    def tiles_of(ref, index, lo, hi):
        return ref[index + (slice(SUBS * (lo + pad), SUBS * (hi + pad)), slice(None))].reshape(hi - lo, SUBS, LANES)

    def put(ref, index, lo, value):
        count = value.shape[0]
        ref[index + (slice(SUBS * (lo + pad), SUBS * (lo + count + pad)), slice(None))] = value.reshape(count * SUBS, LANES)

    half = 0.5 * TIME_STEP
    turn = TIME_STEP * CORIOLIS

    for j in range(steps):
        for lo, hi, mask in pieces(j + 1, span - j - 1):
            h = tiles_of(traj, (j, 0), lo - 1, hi + 1)
            e = tiles_of(traj, (j, 1), lo - 1, hi + 1)
            n = tiles_of(traj, (j, 2), lo - 1, hi + 1)
            h0, e0, n0 = h[1:-1], e[1:-1], n[1:-1]
            hr, er, nr = (next_col(x, last_lane) for x in (h0, e0, n0))
            hl, el, nl = (prev_col(x, first_lane) for x in (h0, e0, n0))
            n_dx = nr - nl
            put(saved, (j, 0), lo, el)
            put(saved, (j, 1), lo, er)
            put(saved, (j, 2), lo, n_dx)
            flux_n = n * h + n
            he = h0 * (1.0 - 4.0 * DIFFUSION) - half * ((er * hr + er) - (el * hl + el) + flux_n[2:] - flux_n[:-2]) + DIFFUSION * (hr + hl + h[2:] + h[:-2])
            ee = e0 * (1.0 - 4.0 * DIFFUSION) - half * ((hr - hl) + e0 * (er - el) + n0 * (e[2:] - e[:-2])) + turn * n0 + DIFFUSION * (er + el + e[2:] + e[:-2])
            ne = n0 * (1.0 - 4.0 * DIFFUSION) - half * ((h[2:] - h[:-2]) + e0 * n_dx + n0 * (n[2:] - n[:-2])) - turn * e0 + DIFFUSION * (nr + nl + n[2:] + n[:-2])
            for f, x in enumerate((he, ee, ne)):
                if mask is not None:
                    x = x * mask
                if j + 1 < steps:
                    put(traj, (j + 1, f), lo, x)
                else:
                    put(end, (f,), lo - steps - pad, x)

    for f in range(fields):
        @pl.when(has_next)
        def _():
            start_back[f].wait_recv()
            if f == 0:
                for copy in end_on:
                    copy.start()
            for g in range(0, rows, SUBS):
                for b in range(SUBS):
                    nw[f, pl.ds(SUBS * g + b, SUBS, stride=SUBS), :] = nxt[f, g:g + SUBS, b * LANES:(b + 1) * LANES]
            nw[f] = weigh(f, nw[f] - end[f])

        @pl.when(jnp.logical_not(has_next))
        def _():
            nw[f] = jnp.zeros((tiles, LANES), jnp.float32)

    own_rows = slice(SUBS * (steps + pad), SUBS * (steps + rows + pad))
    for f in range(fields):
        force = -nw[f]
        if f == 0:
            force = force + (counts[steps - 1] * end[0] - sums[steps - 1])
        lam[0, f, own_rows, :] = force

    for j in range(steps - 1, -1, -1):
        now = (steps - 1 - j) % 2
        later = 1 - now
        for lo, hi, mask in pieces(j, span - j):
            p, q, r = (tiles_of(lam, (now, f), lo - 1, hi + 1) for f in range(3))
            h0 = tiles_of(traj, (j, 0), lo, hi)
            e = tiles_of(traj, (j, 1), lo - 1, hi + 1)
            n = tiles_of(traj, (j, 2), lo - 1, hi + 1)
            el = tiles_of(saved, (j, 0), lo, hi)
            er = tiles_of(saved, (j, 1), lo, hi)
            n_dx = tiles_of(saved, (j, 2), lo, hi)
            e0, n0 = e[1:-1], n[1:-1]
            p0, q0, r0 = p[1:-1], q[1:-1], r[1:-1]
            pr, qr, rr = (next_col(x, last_lane) for x in (p0, q0, r0))
            pl_, ql, rl = (prev_col(x, first_lane) for x in (p0, q0, r0))
            dxp, dyp = pr - pl_, p[2:] - p[:-2]
            qn, rn = q * n, r * n
            ah = p0 * (1.0 - 4.0 * DIFFUSION) + half * (e0 * dxp + n0 * dyp + (qr - ql) + (r[2:] - r[:-2])) + DIFFUSION * (pr + pl_ + p[2:] + p[:-2])
            ae = q0 * (1.0 - 4.0 * DIFFUSION) + half * ((h0 * dxp + dxp) - q0 * (er - el) + (qr * er - ql * el) + (qn[2:] - qn[:-2]) - r0 * n_dx) - turn * r0 + DIFFUSION * (qr + ql + q[2:] + q[:-2])
            an = r0 * (1.0 - 4.0 * DIFFUSION) + half * ((h0 * dyp + dyp) - q0 * (e[2:] - e[:-2]) - r0 * (n[2:] - n[:-2]) + (rr * er - rl * el) + (rn[2:] - rn[:-2])) + turn * q0 + DIFFUSION * (rr + rl + r[2:] + r[:-2])
            if j > 0 and mask is None:
                at = slice(SUBS * (lo - steps), SUBS * (hi - steps))
                shape = (hi - lo, SUBS, LANES)
                ah = ah + (counts[j - 1, at, :].reshape(shape) * h0 - sums[j - 1, at, :].reshape(shape))
            for f, x in enumerate((ah, ae, an)):
                if mask is not None:
                    x = x * mask
                if j == 0 and lo < steps:
                    spill_up[f, SUBS * lo:SUBS * hi, :] = x.reshape((hi - lo) * SUBS, LANES)
                elif j == 0 and lo >= steps + rows:
                    at = slice(SUBS * (lo - steps - rows), SUBS * (hi - steps - rows))
                    spill_down[f, at, :] = x.reshape((hi - lo) * SUBS, LANES)
                else:
                    put(lam, (later, f), lo, x)
            if j == 0 and hi == span:
                @pl.when(has_up)
                def _():
                    spill_to_up.start()

                @pl.when(has_down)
                def _():
                    spill_to_down.start()

    last = steps % 2

    for f in range(fields):
        @pl.when(has_prev)
        def _():
            end_on[f].wait_recv()

        @pl.when(jnp.logical_not(has_prev))
        def _():
            prev_end[f] = jnp.zeros((tiles, LANES), jnp.float32)

        start = traj[0, f, own_rows, :]
        grad[f] = lam[last, f, own_rows, :] + weigh(f, start - prev_end[f])

    @pl.when(has_up)
    def _():
        spill_to_down.wait_recv()
        for f in range(fields):
            at = slice(0, SUBS * steps)
            grad[f, at, :] = grad[f, at, :] + got_top[f]

    @pl.when(has_down)
    def _():
        spill_to_up.wait_recv()
        for f in range(fields):
            at = slice(SUBS * (rows - steps), SUBS * rows)
            grad[f, at, :] = grad[f, at, :] + got_bot[f]

    for there, copies in (
        (has_up, [halo_up, spill_to_up]),
        (has_down, [halo_down, spill_to_down]),
        (has_prev, start_back),
        (has_next, end_on),
    ):
        @pl.when(there)
        def _():
            for copy in copies:
                copy.wait_send()


def finish(tiled, own, grad_hbm, ana_hbm, grad, ana, sems):
    fields, rows, _ = own.shape
    out = []
    for f in range(fields):
        for g in range(0, rows, SUBS):
            for b in range(SUBS):
                value = tiled[f, pl.ds(SUBS * g + b, SUBS, stride=SUBS), :]
                where = (f, slice(g, g + SUBS), slice(b * LANES, (b + 1) * LANES))
                grad[where] = value
                ana[where] = own[where] - STEP_LENGTH * value
        out.append(pltpu.make_async_copy(grad.at[f], grad_hbm.at[0, f], sems.at[2 * f]))
        out.append(pltpu.make_async_copy(ana.at[f], ana_hbm.at[0, f], sems.at[2 * f + 1]))
        out[-2].start()
        out[-1].start()
    for copy in out:
        copy.wait()


def per_device(start_states, obs_cells, obs_values, weighting, live_windows):
    n_win, n_strip = lax.axis_size("win"), lax.axis_size("strip")
    _, fields, rows, cols = start_states.shape
    steps, n_obs = obs_cells.shape[1:]
    span = rows + 2 * steps + 2
    f32 = jnp.float32
    hbm = pl.BlockSpec(memory_space=pl.ANY)
    out = jax.ShapeDtypeStruct(start_states.shape, f32)
    dma = pltpu.SemaphoreType.DMA
    tiled, own = pl.pallas_call(
        functools.partial(kernel, n_win, n_strip),
        out_shape=(pltpu.VMEM((fields, rows * SUBS, LANES), f32), pltpu.VMEM((fields, rows, cols), f32)),
        in_specs=[hbm] * 4 + [pl.BlockSpec(memory_space=pltpu.HBM)],
        out_specs=(pl.BlockSpec(memory_space=pltpu.VMEM),) * 2,
        scratch_shapes=[
            pltpu.VMEM((fields, SUBS, cols), f32),
            pltpu.VMEM((fields, SUBS, cols), f32),
            pltpu.VMEM((fields, rows, cols), f32),
            pltpu.VMEM((fields, rows * SUBS, LANES), f32),
            pltpu.VMEM((steps, n_obs), jnp.int32),
            pltpu.VMEM((steps, n_obs), f32),
            pltpu.VMEM(weighting.shape, f32),
            pltpu.SMEM((1,), jnp.int32),
            pltpu.VMEM((fields, 2 * LANES, 2 * LANES), jnp.bfloat16),
            pltpu.VMEM((steps, fields, span * SUBS, LANES), f32),
            pltpu.VMEM((steps, fields, span * SUBS, LANES), f32),
            pltpu.VMEM((fields, rows * SUBS, LANES), f32),
            pltpu.VMEM((2, fields, span * SUBS, LANES), f32),
            pltpu.VMEM((steps, rows * SUBS, LANES), f32),
            pltpu.VMEM((steps, rows * SUBS, LANES), f32),
            pltpu.VMEM((fields, rows * SUBS, LANES), f32),
            pltpu.VMEM((fields, steps * SUBS, LANES), f32),
            pltpu.VMEM((fields, steps * SUBS, LANES), f32),
            pltpu.VMEM((fields, steps * SUBS, LANES), f32),
            pltpu.VMEM((fields, steps * SUBS, LANES), f32),
            dma((5,)),
            dma((4 + 2 * fields,)),
            dma((4 + 2 * fields,)),
        ],
        compiler_params=pltpu.CompilerParams(collective_id=0, has_side_effects=True),
    )(start_states, obs_cells, obs_values, weighting, live_windows)
    return pl.pallas_call(
        finish,
        out_shape=(out, out),
        in_specs=[pl.BlockSpec(memory_space=pltpu.VMEM)] * 2,
        out_specs=(hbm, hbm),
        scratch_shapes=[pltpu.VMEM((fields, rows, cols), f32)] * 2 + [dma((2 * fields,))],
    )(*(pltpu.with_memory_space_constraint(x, pltpu.VMEM) for x in (tiled, own)))


def solution(mesh):
    placed = (
        P("win", None, "strip", None),
        P("win", None, "strip"),
        P("win", None, "strip"),
        P(),
        P("win"),
    )
    return jax.shard_map(
        per_device,
        mesh=mesh,
        in_specs=placed,
        out_specs=(P("win", None, "strip", None), P("win", None, "strip", None)),
        check_vma=False,
    )
```

```python
import functools

import jax
import jax.numpy as jnp
from jax import lax
from jax.experimental import pallas as pl
from jax.experimental.pallas import tpu as pltpu
from jax.sharding import PartitionSpec as P

TIME_STEP = 0.2
DIFFUSION = 0.12
CORIOLIS = 0.5
STEP_LENGTH = 0.5
LANES = 128
SUBS = 8
CHUNK = 2


def next_col(x, last_lane):
    turned = pltpu.roll(x, LANES - 1, 2)
    return jnp.where(last_lane, pltpu.roll(turned, SUBS - 1, 1), turned)


def prev_col(x, first_lane):
    turned = pltpu.roll(x, 1, 2)
    return jnp.where(first_lane, pltpu.roll(turned, 1, 1), turned)


def kernel(
    n_win, n_strip,
    start_hbm, cells_hbm, values_hbm, weight_hbm, live_hbm,
    grad, own,
    above, below, nxt, prev_end, cells, values, weight, live,
    rhs, traj, saved, end, lam, counts, sums, nw, spill_up, spill_down, got_top, got_bot,
    local_sem, send_sem, recv_sem,
):
    fields, rows, cols = own.shape
    steps = cells.shape[0]
    span = rows + 2 * steps
    pad = 1
    win, strip = lax.axis_index("win"), lax.axis_index("strip")
    has_prev, has_next = win > 0, win < n_win - 1
    has_up, has_down = strip > 0, strip < n_strip - 1

    def at_win(by):
        return {"win": jnp.clip(win + by, 0, n_win - 1)}

    def at_strip(by):
        return {"strip": jnp.clip(strip + by, 0, n_strip - 1)}

    loads = [
        pltpu.make_async_copy(start_hbm.at[0], own, local_sem.at[0]),
        pltpu.make_async_copy(cells_hbm.at[0], cells, local_sem.at[1]),
        pltpu.make_async_copy(values_hbm.at[0], values, local_sem.at[2]),
        pltpu.make_async_copy(weight_hbm, weight, local_sem.at[3]),
        pltpu.make_async_copy(live_hbm, live, local_sem.at[4]),
    ]
    barrier = pltpu.get_barrier_semaphore()
    for there, peer in ((has_up, at_strip(-1)), (has_down, at_strip(1)), (has_prev, at_win(-1)), (has_next, at_win(1))):
        @pl.when(there)
        def _():
            pl.semaphore_signal(barrier, inc=1, device_id=peer, device_id_type=pl.DeviceIdType.MESH)
    for load in loads:
        load.start()

    pl.semaphore_wait(barrier, sum(there.astype(jnp.int32) for there in (has_up, has_down, has_prev, has_next)))

    def remote(src, dst, sem, peer):
        return pltpu.make_async_remote_copy(
            src_ref=src, dst_ref=dst, send_sem=send_sem.at[sem], recv_sem=recv_sem.at[sem],
            device_id=peer, device_id_type=pl.DeviceIdType.MESH,
        )

    halo_up = remote(start_hbm.at[0, :, 0:SUBS, :], below, 0, at_strip(-1))
    halo_down = remote(start_hbm.at[0, :, rows - SUBS:rows, :], above, 1, at_strip(1))
    start_back = [remote(start_hbm.at[0, f], nxt.at[f], 2 + f, at_win(-1)) for f in range(fields)]
    end_on = [remote(end.at[f], prev_end.at[f], 2 + fields + f, at_win(1)) for f in range(fields)]
    spill_to_up = remote(spill_up, got_bot, 2 + 2 * fields, at_strip(-1))
    spill_to_down = remote(spill_down, got_top, 3 + 2 * fields, at_strip(1))

    @pl.when(has_prev)
    def _():
        for copy in start_back:
            copy.start()

    @pl.when(has_up)
    def _():
        halo_up.start()

    @pl.when(has_down)
    def _():
        halo_down.start()

    lane = lax.broadcasted_iota(jnp.int32, (1, SUBS, LANES), 2)
    first_lane, last_lane = lane == 0, lane == LANES - 1
    zero_row = jnp.zeros((SUBS, LANES), jnp.float32)

    for buf in range(2):
        for f in range(fields):
            for row in list(range(0, steps + pad)) + list(range(steps + pad + rows, span + 2 * pad)):
                lam[buf, f, SUBS * row:SUBS * (row + 1), :] = zero_row
    for j in range(steps):
        for row in (j - 1 + pad, span - j + pad):
            for f in range(fields):
                traj[j, f, SUBS * row:SUBS * (row + 1), :] = zero_row
        for row in (j + pad, span - j - 1 + pad):
            for f in range(fields):
                saved[j, f, SUBS * row:SUBS * (row + 1), :] = zero_row

    loads[0].wait()
    for f in range(fields):
        for g in range(0, rows, SUBS):
            for b in range(SUBS):
                base = SUBS * (steps + pad + g) + b
                traj[0, f, pl.ds(base, SUBS, stride=SUBS), :] = own[f, g:g + SUBS, b * LANES:(b + 1) * LANES]

    loads[1].wait()
    loads[2].wait()
    loads[4].wait()
    alive = live[0].astype(jnp.float32)
    n_obs = cells.shape[1]
    tiles = rows * SUBS
    tile_id = lax.broadcasted_iota(jnp.int32, (tiles, n_obs), 0)
    lane_id = lax.broadcasted_iota(jnp.int32, (LANES, n_obs), 0)
    for j in range(steps):
        cell = cells[j:j + 1, :]
        value = values[j:j + 1, :]
        in_tile = tile_id == lax.shift_right_logical(cell, 7)
        in_lane = lane_id == (cell & (LANES - 1))
        high = value.astype(jnp.bfloat16).astype(jnp.float32)
        low = value - high
        picks = jnp.concatenate(
            [
                jnp.where(in_tile, 1.0, 0.0).astype(jnp.bfloat16),
                jnp.where(in_tile, high, 0.0).astype(jnp.bfloat16),
                jnp.where(in_tile, low, 0.0).astype(jnp.bfloat16),
            ],
            axis=0,
        )
        dense = lax.dot_general(
            picks, jnp.where(in_lane, 1.0, 0.0).astype(jnp.bfloat16),
            (((1,), (1,)), ((), ())), preferred_element_type=jnp.float32,
        )
        counts[j] = alive * dense[:tiles]
        sums[j] = alive * (dense[tiles:2 * tiles] + dense[2 * tiles:])

    loads[3].wait()
    for f in range(fields):
        w = weight[f]
        w_high = w.astype(jnp.bfloat16)
        w_low = (w - w_high.astype(jnp.float32)).astype(jnp.bfloat16)
        rhs[f, 0:LANES, 0:LANES] = w_high
        rhs[f, 0:LANES, LANES:] = w_low
        rhs[f, LANES:, 0:LANES] = w_high
        rhs[f, LANES:, LANES:] = jnp.zeros_like(w_low)

    def weigh(f, defect):
        high = defect.astype(jnp.bfloat16)
        low = (defect - high.astype(jnp.float32)).astype(jnp.bfloat16)
        out = jnp.dot(jnp.concatenate([high, low], axis=1), rhs[f], preferred_element_type=jnp.float32)
        return defect + (out[:, :LANES] + out[:, LANES:])

    for there, copy, src, src_row, dst_row in (
        (has_up, halo_down, above, SUBS - steps, pad),
        (has_down, halo_up, below, 0, pad + steps + rows),
    ):
        @pl.when(there)
        def _():
            copy.wait_recv()
            for f in range(fields):
                for b in range(SUBS):
                    base = SUBS * dst_row + b
                    traj[0, f, pl.ds(base, steps, stride=SUBS), :] = src[f, src_row:src_row + steps, b * LANES:(b + 1) * LANES]

        @pl.when(jnp.logical_not(there))
        def _():
            for f in range(fields):
                traj[0, f, SUBS * dst_row:SUBS * (dst_row + steps), :] = jnp.zeros((SUBS * steps, LANES), jnp.float32)

    up_mask = jnp.where(has_up, 1.0, 0.0).astype(jnp.float32)
    down_mask = jnp.where(has_down, 1.0, 0.0).astype(jnp.float32)

    def pieces(lo, hi):
        edges = []
        for a, b, mask in ((lo, min(hi, steps), up_mask), (steps + rows, hi, down_mask), (steps, steps + rows, None)):
            for r in range(a, b, CHUNK):
                edges.append((r, min(r + CHUNK, b), mask))
        return edges

    def tiles_of(ref, index, lo, hi):
        return ref[index + (slice(SUBS * (lo + pad), SUBS * (hi + pad)), slice(None))].reshape(hi - lo, SUBS, LANES)

    def put(ref, index, lo, value):
        count = value.shape[0]
        ref[index + (slice(SUBS * (lo + pad), SUBS * (lo + count + pad)), slice(None))] = value.reshape(count * SUBS, LANES)

    half = 0.5 * TIME_STEP
    turn = TIME_STEP * CORIOLIS

    for j in range(steps):
        for lo, hi, mask in pieces(j + 1, span - j - 1):
            h = tiles_of(traj, (j, 0), lo - 1, hi + 1)
            e = tiles_of(traj, (j, 1), lo - 1, hi + 1)
            n = tiles_of(traj, (j, 2), lo - 1, hi + 1)
            h0, e0, n0 = h[1:-1], e[1:-1], n[1:-1]
            hr, er, nr = (next_col(x, last_lane) for x in (h0, e0, n0))
            hl, el, nl = (prev_col(x, first_lane) for x in (h0, e0, n0))
            n_dx = nr - nl
            put(saved, (j, 0), lo, el)
            put(saved, (j, 1), lo, er)
            put(saved, (j, 2), lo, n_dx)
            flux_n = n * h + n
            he = h0 * (1.0 - 4.0 * DIFFUSION) - half * ((er * hr + er) - (el * hl + el) + flux_n[2:] - flux_n[:-2]) + DIFFUSION * (hr + hl + h[2:] + h[:-2])
            ee = e0 * (1.0 - 4.0 * DIFFUSION) - half * ((hr - hl) + e0 * (er - el) + n0 * (e[2:] - e[:-2])) + turn * n0 + DIFFUSION * (er + el + e[2:] + e[:-2])
            ne = n0 * (1.0 - 4.0 * DIFFUSION) - half * ((h[2:] - h[:-2]) + e0 * n_dx + n0 * (n[2:] - n[:-2])) - turn * e0 + DIFFUSION * (nr + nl + n[2:] + n[:-2])
            for f, x in enumerate((he, ee, ne)):
                if mask is not None:
                    x = x * mask
                if j + 1 < steps:
                    put(traj, (j + 1, f), lo, x)
                else:
                    put(end, (f,), lo - steps - pad, x)

    for f in range(fields):
        @pl.when(has_next)
        def _():
            start_back[f].wait_recv()
            if f < 2:
                @pl.when(win % 2 == 1 - f)
                def _():
                    for copy in end_on:
                        copy.start()
            for g in range(0, rows, SUBS):
                for b in range(SUBS):
                    nw[f, pl.ds(SUBS * g + b, SUBS, stride=SUBS), :] = nxt[f, g:g + SUBS, b * LANES:(b + 1) * LANES]
            nw[f] = weigh(f, nw[f] - end[f])

        @pl.when(jnp.logical_not(has_next))
        def _():
            nw[f] = jnp.zeros((tiles, LANES), jnp.float32)

    own_rows = slice(SUBS * (steps + pad), SUBS * (steps + rows + pad))
    for f in range(fields):
        force = -nw[f]
        if f == 0:
            force = force + (counts[steps - 1] * end[0] - sums[steps - 1])
        lam[0, f, own_rows, :] = force

    for j in range(steps - 1, -1, -1):
        now = (steps - 1 - j) % 2
        later = 1 - now
        for lo, hi, mask in pieces(j, span - j):
            p, q, r = (tiles_of(lam, (now, f), lo - 1, hi + 1) for f in range(3))
            h0 = tiles_of(traj, (j, 0), lo, hi)
            e = tiles_of(traj, (j, 1), lo - 1, hi + 1)
            n = tiles_of(traj, (j, 2), lo - 1, hi + 1)
            el = tiles_of(saved, (j, 0), lo, hi)
            er = tiles_of(saved, (j, 1), lo, hi)
            n_dx = tiles_of(saved, (j, 2), lo, hi)
            e0, n0 = e[1:-1], n[1:-1]
            p0, q0, r0 = p[1:-1], q[1:-1], r[1:-1]
            pr, qr, rr = (next_col(x, last_lane) for x in (p0, q0, r0))
            pl_, ql, rl = (prev_col(x, first_lane) for x in (p0, q0, r0))
            dxp, dyp = pr - pl_, p[2:] - p[:-2]
            qn, rn = q * n, r * n
            ah = p0 * (1.0 - 4.0 * DIFFUSION) + half * (e0 * dxp + n0 * dyp + (qr - ql) + (r[2:] - r[:-2])) + DIFFUSION * (pr + pl_ + p[2:] + p[:-2])
            ae = q0 * (1.0 - 4.0 * DIFFUSION) + half * ((h0 * dxp + dxp) - q0 * (er - el) + (qr * er - ql * el) + (qn[2:] - qn[:-2]) - r0 * n_dx) - turn * r0 + DIFFUSION * (qr + ql + q[2:] + q[:-2])
            an = r0 * (1.0 - 4.0 * DIFFUSION) + half * ((h0 * dyp + dyp) - q0 * (e[2:] - e[:-2]) - r0 * (n[2:] - n[:-2]) + (rr * er - rl * el) + (rn[2:] - rn[:-2])) + turn * q0 + DIFFUSION * (rr + rl + r[2:] + r[:-2])
            if j > 0 and mask is None:
                at = slice(SUBS * (lo - steps), SUBS * (hi - steps))
                shape = (hi - lo, SUBS, LANES)
                ah = ah + (counts[j - 1, at, :].reshape(shape) * h0 - sums[j - 1, at, :].reshape(shape))
            for f, x in enumerate((ah, ae, an)):
                if mask is not None:
                    x = x * mask
                if j == 0 and lo < steps:
                    spill_up[f, SUBS * lo:SUBS * hi, :] = x.reshape((hi - lo) * SUBS, LANES)
                elif j == 0 and lo >= steps + rows:
                    at = slice(SUBS * (lo - steps - rows), SUBS * (hi - steps - rows))
                    spill_down[f, at, :] = x.reshape((hi - lo) * SUBS, LANES)
                else:
                    put(lam, (later, f), lo, x)
            if j == 0 and hi == span:
                @pl.when(has_up)
                def _():
                    spill_to_up.start()

                @pl.when(has_down)
                def _():
                    spill_to_down.start()

    last = steps % 2

    @pl.when(has_up)
    def _():
        spill_to_down.wait_recv()
        for f in range(fields):
            at = slice(SUBS * (steps + pad), SUBS * (2 * steps + pad))
            lam[last, f, at, :] = lam[last, f, at, :] + got_top[f]

    @pl.when(has_down)
    def _():
        spill_to_up.wait_recv()
        for f in range(fields):
            at = slice(SUBS * (rows + pad), SUBS * (steps + rows + pad))
            lam[last, f, at, :] = lam[last, f, at, :] + got_bot[f]

    for f in range(fields):
        @pl.when(has_prev)
        def _():
            end_on[f].wait_recv()

        @pl.when(jnp.logical_not(has_prev))
        def _():
            prev_end[f] = jnp.zeros((tiles, LANES), jnp.float32)

        start = traj[0, f, own_rows, :]
        grad[f] = lam[last, f, own_rows, :] + weigh(f, start - prev_end[f])

    for there, copies in (
        (has_up, [halo_up, spill_to_up]),
        (has_down, [halo_down, spill_to_down]),
        (has_prev, start_back),
        (has_next, end_on),
    ):
        @pl.when(there)
        def _():
            for copy in copies:
                copy.wait_send()


def finish(tiled, own, grad_hbm, ana_hbm, grad, ana, sems):
    fields, rows, _ = own.shape
    out = []
    for f in range(fields):
        for g in range(0, rows, SUBS):
            for b in range(SUBS):
                value = tiled[f, pl.ds(SUBS * g + b, SUBS, stride=SUBS), :]
                where = (f, slice(g, g + SUBS), slice(b * LANES, (b + 1) * LANES))
                grad[where] = value
                ana[where] = own[where] - STEP_LENGTH * value
        out.append(pltpu.make_async_copy(grad.at[f], grad_hbm.at[0, f], sems.at[2 * f]))
        out.append(pltpu.make_async_copy(ana.at[f], ana_hbm.at[0, f], sems.at[2 * f + 1]))
        out[-2].start()
        out[-1].start()
    for copy in out:
        copy.wait()


def per_device(start_states, obs_cells, obs_values, weighting, live_windows):
    n_win, n_strip = lax.axis_size("win"), lax.axis_size("strip")
    _, fields, rows, cols = start_states.shape
    steps, n_obs = obs_cells.shape[1:]
    span = rows + 2 * steps + 2
    f32 = jnp.float32
    hbm = pl.BlockSpec(memory_space=pl.ANY)
    out = jax.ShapeDtypeStruct(start_states.shape, f32)
    dma = pltpu.SemaphoreType.DMA
    tiled, own = pl.pallas_call(
        functools.partial(kernel, n_win, n_strip),
        out_shape=(pltpu.VMEM((fields, rows * SUBS, LANES), f32), pltpu.VMEM((fields, rows, cols), f32)),
        in_specs=[hbm] * 4 + [pl.BlockSpec(memory_space=pltpu.HBM)],
        out_specs=(pl.BlockSpec(memory_space=pltpu.VMEM),) * 2,
        scratch_shapes=[
            pltpu.VMEM((fields, SUBS, cols), f32),
            pltpu.VMEM((fields, SUBS, cols), f32),
            pltpu.VMEM((fields, rows, cols), f32),
            pltpu.VMEM((fields, rows * SUBS, LANES), f32),
            pltpu.VMEM((steps, n_obs), jnp.int32),
            pltpu.VMEM((steps, n_obs), f32),
            pltpu.VMEM(weighting.shape, f32),
            pltpu.SMEM((1,), jnp.int32),
            pltpu.VMEM((fields, 2 * LANES, 2 * LANES), jnp.bfloat16),
            pltpu.VMEM((steps, fields, span * SUBS, LANES), f32),
            pltpu.VMEM((steps, fields, span * SUBS, LANES), f32),
            pltpu.VMEM((fields, rows * SUBS, LANES), f32),
            pltpu.VMEM((2, fields, span * SUBS, LANES), f32),
            pltpu.VMEM((steps, rows * SUBS, LANES), f32),
            pltpu.VMEM((steps, rows * SUBS, LANES), f32),
            pltpu.VMEM((fields, rows * SUBS, LANES), f32),
            pltpu.VMEM((fields, steps * SUBS, LANES), f32),
            pltpu.VMEM((fields, steps * SUBS, LANES), f32),
            pltpu.VMEM((fields, steps * SUBS, LANES), f32),
            pltpu.VMEM((fields, steps * SUBS, LANES), f32),
            dma((5,)),
            dma((4 + 2 * fields,)),
            dma((4 + 2 * fields,)),
        ],
        compiler_params=pltpu.CompilerParams(collective_id=0, has_side_effects=True),
    )(start_states, obs_cells, obs_values, weighting, live_windows)
    return pl.pallas_call(
        finish,
        out_shape=(out, out),
        in_specs=[pl.BlockSpec(memory_space=pltpu.VMEM)] * 2,
        out_specs=(hbm, hbm),
        scratch_shapes=[pltpu.VMEM((fields, rows, cols), f32)] * 2 + [dma((2 * fields,))],
    )(*(pltpu.with_memory_space_constraint(x, pltpu.VMEM) for x in (tiled, own)))


def solution(mesh):
    placed = (
        P("win", None, "strip", None),
        P("win", None, "strip"),
        P("win", None, "strip"),
        P(),
        P("win"),
    )
    return jax.shard_map(
        per_device,
        mesh=mesh,
        in_specs=placed,
        out_specs=(P("win", None, "strip", None), P("win", None, "strip", None)),
        check_vma=False,
    )
```
